32 devices in a mesh: board: 16 (over z, y, x), hand: 2 (over core).
Axes of the slice: x: 2, y: 2, z: 4, core: 2. Of those that a mesh axis runs over, the one named last changes fastest.
Arguments:
- opp_reach: bfloat16 [1024, 1326], P('board', 'hand'), may hold values from 0.019897461 to 1
- hand_rank: int32 [1024, 1326], P('board'), may hold values from 0 to 1325, as said below
- hand_cards: int32 [1326, 2], replicated, may hold values from 0 to 51, as said below
- pot: float32 [1024], P('board'), may hold values from 1 to 12
- bet_frac: float32 [1024], P('board'), may hold values from 0.25 to 1.5
- trav_reach: float32 [1326], P('hand'), may hold values from 0.02 to 1
Outputs:
- board_values: float32 [1024, 1326], P('board', 'hand')
- hand_values: float32 [1326], P('hand')
- exploitability: float32 [], replicated
The draws below stay inside these ranges and needn't reach their ends.
Inputs may be any that keep to these rules, and one draw needn't show every extreme that they name: hand_rank[b, i] is the number of hands strictly weaker than hand i on board b; equal ranks tie. `hand_cards`: the rows are the 1326 distinct pairs of two different cards, smaller card first, in an order drawn from the seed.
All inputs are finite; a program needn't handle non-finite values.
Results may differ from the reference program's by a relative error of at most 0.0003.
Values may be sent and summed in bfloat16 or wider, within the bound.
A program may use at most 64 MiB of HBM per device.

```python
import math
import jax
import jax.numpy as jnp
import numpy as np
from jax import lax

CARDS = 52
H = 1326
BOARDS = 1024


def showdown_order(key):
    seeded = jax.random.fold_in(key, 7)
    hand_key, board_key = jax.random.split(seeded)
    strength = jax.random.randint(hand_key, (1, H), 0, 3 * H // 4)
    noise = jax.random.randint(board_key, (BOARDS, H), 0, H // 2)
    scores = (strength + noise).astype(jnp.int32)
    ordering = jnp.argsort(scores, axis=1, stable=True).astype(jnp.int32)
    ranked = jnp.take_along_axis(scores, ordering, axis=1)
    positions = lax.broadcasted_iota(jnp.int32, (BOARDS, H), 1)
    fresh = jnp.concatenate([jnp.ones((BOARDS, 1), jnp.bool_), ranked[:, 1:] != ranked[:, :-1]], axis=1)
    starts = lax.cummax(jnp.where(fresh, positions, 0), axis=1)
    board_rows = lax.broadcasted_iota(jnp.int32, (BOARDS, H), 0)
    rank_table = jnp.zeros((BOARDS, H), jnp.int32).at[board_rows, ordering].set(starts)
    return rank_table


def draw_hand_rank(key, part):
    return showdown_order(key)


def draw_hand_cards(key, part):
    lower_card, upper_card = np.triu_indices(CARDS, 1)
    pairs = jnp.stack([jnp.asarray(lower_card), jnp.asarray(upper_card)], axis=1).astype(jnp.int32)
    shuffle = jax.random.permutation(jax.random.fold_in(key, 11), H)
    return pairs[shuffle]


def draw_pot(key, part):
    seeded = jax.random.fold_in(key, 13)
    spread = jnp.arange(BOARDS, dtype=jnp.float32) / max(BOARDS - 1, 1)
    level = jnp.exp(jax.random.uniform(seeded, (BOARDS,), jnp.float32, 0.0, math.log(4.0)))
    return ((1.0 + 2.0 * spread) * level).astype(jnp.float32)


def shard_levels(stream_key, extent, pieces, low, top_value):
    level, own = 1.0, jax.random.fold_in(stream_key, 6)
    for position, parts in pieces:
        steps = jnp.exp(jax.random.uniform(jax.random.fold_in(own, position), (parts,), jnp.float32, low / len(pieces), top_value / len(pieces)))
        level = level * jnp.repeat(steps, extent[position] // parts).reshape([-1 if axis == position else 1 for axis in range(len(extent))])
    return level


def setup_inputs(seed: int = 0) -> dict:
    streams_of = jax.random.split(jax.random.key(seed), 7)
    return {
        "opp_reach": jnp.clip(jnp.exp(math.log(1.0) - 3.9171631 * jax.random.uniform(streams_of[0], (BOARDS, H), jnp.float32) ** shard_levels(streams_of[0], (BOARDS, H), ((0, 16), (1, 2)), -0.2, 0.2)), 0.019897461, 1.0).astype(jnp.bfloat16),
        "hand_rank": draw_hand_rank(jax.random.fold_in(streams_of[6], 71), 0),
        "hand_cards": draw_hand_cards(jax.random.fold_in(streams_of[6], 71), 0),
        "pot": draw_pot(jax.random.fold_in(streams_of[6], 71), 0),
        "bet_frac": jnp.clip(0.25 + 1.25 * jax.random.uniform(streams_of[4], (BOARDS,), jnp.float32) ** shard_levels(streams_of[4], (BOARDS,), ((0, 16),), -0.2, 0.2), 0.25, 1.5),
        "trav_reach": jnp.clip(jnp.exp(math.log(1.0) - 3.912023 * jax.random.uniform(streams_of[5], (H,), jnp.float32) ** shard_levels(streams_of[5], (H,), ((0, 2),), -0.2, 0.2)), 0.02, 1.0),
    }


def incidence(hand_cards):
    card_ids = jnp.arange(CARDS, dtype=jnp.int32)
    return ((hand_cards[:, 0:1] == card_ids) | (hand_cards[:, 1:2] == card_ids)).astype(jnp.float32)


def showdown(opp_reach, hand_rank, hand_cards):
    card_hold = incidence(hand_cards)
    first_card = hand_cards[:, 0]
    second_card = hand_cards[:, 1]
    positions = jnp.arange(H, dtype=jnp.int32)

    def one_board(board_data):
        rank_row, reach_row = board_data
        order_row = jnp.argsort(rank_row, stable=True).astype(jnp.int32)
        own_reach = reach_row.astype(jnp.float32)
        weighted = own_reach[:, None] * card_hold
        ordered = weighted[order_row]
        prefix = jnp.concatenate([jnp.zeros((1, CARDS), jnp.float32), jnp.cumsum(ordered, axis=0)], axis=0)
        share = jnp.sum(prefix, axis=1) * 0.5
        sorted_rank = rank_row[order_row]
        group_marks = jnp.where(sorted_rank == positions, positions, H)
        shifted = jnp.concatenate([group_marks[1:], jnp.full((1,), H, jnp.int32)])
        next_start = lax.cummin(shifted, axis=0, reverse=True)
        tie_end = next_start[rank_row]

        def blocked(row_index):
            return share[row_index] - prefix[row_index, first_card] - prefix[row_index, second_card]

        beaten = blocked(rank_row)
        reached = blocked(tie_end) + own_reach
        live_mass = blocked(jnp.full((H,), H, jnp.int32)) + own_reach
        return beaten + reached - live_mass, live_mass

    return lax.map(one_board, (hand_rank, opp_reach))


def reference(opp_reach, hand_rank, hand_cards, pot, bet_frac, trav_reach):
    margin, live_mass = showdown(opp_reach, hand_rank, hand_cards)
    half_pot = (0.5 * pot)[:, None]
    call_value = (half_pot + (bet_frac * pot)[:, None]) * margin / H
    fold_value = -half_pot * live_mass / H
    board_values = jnp.maximum(call_value, fold_value)
    hand_values = jnp.mean(board_values, axis=0)
    opp_mass = jnp.mean(half_pot * live_mass / H, axis=0)
    exploit = jnp.sum(trav_reach * hand_values) / jnp.sum(trav_reach * opp_mass)
    return board_values, hand_values, exploit
```

```python
import functools

import jax
import jax.numpy as jnp
from jax import lax
from jax.experimental import pallas as pl
from jax.experimental.pallas import tpu as pltpu
from jax.sharding import PartitionSpec as P

CARDS = 52
LANES = 128
STRIDE = 64
DIGIT = 32
MESH = pl.DeviceIdType.MESH
F32 = jnp.float32
BF16 = jnp.bfloat16
NT = (((1,), (1,)), ((), ()))


def up(n, m):
    return (n + m - 1) // m * m


def iota(shape, axis, dtype=jnp.int32):
    return lax.broadcasted_iota(jnp.int32, shape, axis).astype(dtype)


def column(row):
    n = row.shape[1]
    diag = iota((n, n), 0) == iota((n, n), 1)
    return jnp.sum(jnp.where(diag, row, 0.0), axis=1, keepdims=True)


def split2(x):
    top = x.astype(BF16)
    return top, (x - top.astype(F32)).astype(BF16)


def split3(x):
    top = x.astype(BF16)
    rest = x - top.astype(F32)
    mid, low = split2(rest)
    return top, mid, low


def kernel(
    nb, opp, rank, cards, pot, bet, trav, bv_out, hv_out, ex_out,
    pt, key, rhi, rlo, wf, xs, got, tt, wt, st, eqs, c1, rt, gg, ct, mm, sb, msg, recva, recvb,
    s_reach, s_ct, s_m, send_a, recv_a, send_b, recv_b,
):
    me, h = lax.axis_index("board"), lax.axis_index("hand")
    boards, half = opp.shape
    hands = rank.shape[1]
    own = boards // 2
    hp = wf.shape[1]
    halfp = mm.shape[1]
    mine = pl.multiple_of(h * own, own)
    theirs = pl.multiple_of((1 - h) * own, own)
    partner = (me, 1 - h)
    pairs = CARDS // 2
    group = LANES // own
    blocks = tt.shape[0]
    left = h == 0

    barrier = pltpu.get_barrier_semaphore()
    for k in range(nb):
        peer = lax.rem(me + k, nb)
        if k:
            pl.semaphore_signal(barrier, inc=1, device_id=(peer, h), device_id_type=MESH)
        pl.semaphore_signal(barrier, inc=1, device_id=(peer, 1 - h), device_id_type=MESH)

    key[...] = jnp.full(key.shape, -1, jnp.int32)
    key[:, :hands] = cards[...]
    u, v = key[0:1, :], key[1:2, :]
    rows = rank[pl.ds(mine, own), :]
    rhi[...] = jnp.zeros(rhi.shape, F32)
    rlo[...] = jnp.zeros(rlo.shape, F32)
    rhi[:, :hands] = (rows // DIGIT).astype(F32)
    rlo[:, :hands] = (rows % DIGIT).astype(F32)

    depth = iota((STRIDE, hp), 0, F32).astype(BF16)

    def build(c, carry):
        other = jnp.where(u == c, v, jnp.where(v == c, u, -1)).astype(F32).astype(BF16)
        hit = depth == jnp.broadcast_to(other, (STRIDE, hp))
        start = pl.multiple_of(c * STRIDE, STRIDE)
        pt[pl.ds(start, STRIDE), :] = jnp.where(hit, jnp.ones((), BF16), jnp.zeros((), BF16))
        return carry

    lax.fori_loop(0, CARDS, build, 0)

    pl.semaphore_wait(barrier, 2 * nb - 1)
    reach_copy = pltpu.make_async_remote_copy(
        src_ref=opp.at[pl.ds(theirs, own)], dst_ref=got, send_sem=s_reach.at[0], recv_sem=s_reach.at[1],
        device_id=partner, device_id_type=MESH,
    )
    reach_copy.start()

    card_row = iota((LANES, hp), 0)
    hold = ((card_row == u) | (card_row == v)).astype(F32).astype(BF16)
    shift = hp - half
    u_r, v_r = pltpu.roll(key[...], shift, 1)[0:1, :halfp], pltpu.roll(key[...], shift, 1)[1:2, :halfp]
    u_m = jnp.where(left, u[:, :halfp], u_r)
    v_m = jnp.where(left, v[:, :halfp], v_r)
    card_half = iota((LANES, halfp), 0)
    hold_m = ((card_half == u_m) | (card_half == v_m)).astype(F32).astype(BF16)

    reach_copy.wait()
    here, there = opp[pl.ds(mine, own), :].astype(F32), got[...].astype(F32)
    wf[...] = jnp.zeros(wf.shape, F32)
    wf[:, :half] = jnp.where(left, there, here)
    second = pltpu.roll(wf[...], half, 1)
    wf[...] = jnp.zeros(wf.shape, F32)
    wf[:, :half] = jnp.where(left, here, there)
    w_all = wf[...] + second
    wf[...] = w_all
    w_low = w_all.astype(BF16)

    ct[pl.ds(mine, own), :] = lax.dot_general(w_low, hold, NT, preferred_element_type=F32)
    ct_copy = pltpu.make_async_remote_copy(
        src_ref=ct.at[pl.ds(mine, own)], dst_ref=ct.at[pl.ds(mine, own)], send_sem=s_ct.at[0], recv_sem=s_ct.at[1],
        device_id=partner, device_id_type=MESH,
    )
    ct_copy.start()

    xs[0:own, :] = rhi[...].astype(BF16)
    xs[own : 2 * own, :] = rlo[...].astype(BF16)
    xs[2 * own :, :] = w_low
    table = lax.dot_general(xs[...], pt[...], NT, preferred_element_type=F32)
    t_tab = table[0:own] * float(DIGIT) + table[own : 2 * own]
    w_tab = table[2 * own :]
    for blk in range(blocks):
        for src, dst in ((t_tab, tt), (w_tab, wt)):
            parts = []
            for q in range(group):
                p = blk * group + q
                if p < pairs:
                    parts.append(src[:, p * LANES : (p + 1) * LANES])
                else:
                    parts.append(jnp.zeros((own, LANES), F32))
            dst[blk] = jnp.concatenate(parts, axis=0).T

    used = up(CARDS, 8)
    st[...] = jnp.zeros(st.shape, F32)

    def correct(n, carry):
        blk, off = n // 2, pl.multiple_of((n % 2) * STRIDE, STRIDE)
        t_here = tt[blk, pl.ds(off, used), :]
        acc = jnp.zeros((used, LANES), F32)
        for e in range(CARDS):
            te = tt[blk, pl.ds(off + e, 1), :]
            we = wt[blk, pl.ds(off + e, 1), :]
            acc = acc + jnp.where(t_here > te, we, jnp.where(t_here < te, -we, 0.0))
        st[blk, pl.ds(off, used), :] = acc
        return carry

    lax.fori_loop(0, 2 * blocks, correct, 0)
    pieces = []
    for p in range(pairs):
        blk, q = p // group, p % group
        if q == 0:
            back = st[blk].T
        pieces.append(back[q * own : (q + 1) * own])
    s_tab = jnp.concatenate(pieces, axis=1)
    s_top, s_low = split2(s_tab)
    scattered = jnp.dot(jnp.concatenate([s_top, s_low], axis=0), pt[...], preferred_element_type=F32)
    corr = scattered[:own] + scattered[own:]

    nhi = c1.shape[2] // 2
    nlo = c1.shape[1]
    hi_row = iota((nhi, hp), 0, F32).astype(BF16)
    lo_row = iota((nlo, hp), 0, F32).astype(BF16)

    def hist(b, carry):
        hi_b = jnp.broadcast_to(rhi[pl.ds(b, 1), :].astype(BF16), (nhi, hp))
        lo_b = jnp.broadcast_to(rlo[pl.ds(b, 1), :].astype(BF16), (nlo, hp))
        w_b = jnp.broadcast_to(wf[pl.ds(b, 1), :].astype(BF16), (nlo, hp))
        eq = jnp.where(hi_row == hi_b, jnp.ones((), BF16), jnp.zeros((), BF16))
        eqs[b, 0:nhi, :] = eq
        eqs[b, nhi : 2 * nhi, :] = eq
        lw = jnp.where(lo_row > lo_b, w_b, jnp.where(lo_row < lo_b, -w_b, jnp.zeros((), BF16)))
        part = lax.dot_general(lw, jnp.concatenate([eq, eq], axis=0), NT, preferred_element_type=F32)
        c1[b] = part
        rt[pl.ds(b, 1), :] = part[DIGIT : DIGIT + 1, :]
        return carry

    lax.fori_loop(0, own, hist, 0, unroll=4)
    wide = 2 * nhi
    a, z = iota((wide, wide), 0), iota((wide, wide), 1)
    z = jnp.where(z >= nhi, z - nhi, z)
    sgn = jnp.where(a >= nhi, 0, jnp.where(z > a, 1, jnp.where(z < a, -1, 0))).astype(F32).astype(BF16)
    r0, r1, r2 = split3(rt[...])
    rt[...] = (
        jnp.dot(r0, sgn, preferred_element_type=F32)
        + jnp.dot(r1, sgn, preferred_element_type=F32)
        + jnp.dot(r2, sgn, preferred_element_type=F32)
    )
    lo_f = iota((DIGIT, hp), 0, F32)
    first = iota((DIGIT, wide), 1) < nhi

    def pick(b, carry):
        tab = c1[b, 0:DIGIT, :] + rt[pl.ds(b, 1), :]
        top = tab.astype(BF16).astype(F32)
        lhs = jnp.where(first, top, tab - top).astype(BF16)
        d = jnp.dot(lhs, eqs[b], preferred_element_type=F32)
        hit = lo_f == rlo[pl.ds(b, 1), :]
        gg[pl.ds(b, 1), :] = jnp.sum(jnp.where(hit, d, 0.0), axis=0, keepdims=True)
        return carry

    lax.fori_loop(0, own, pick, 0, unroll=4)
    margin = gg[...] - corr

    m_left = margin[:, :halfp]
    m_right = pltpu.roll(margin, shift, 1)[:, :halfp]
    sb[...] = jnp.where(left, m_right, m_left)
    m_copy = pltpu.make_async_remote_copy(
        src_ref=sb, dst_ref=mm.at[pl.ds(mine, own)], send_sem=s_m.at[0], recv_sem=s_m.at[1],
        device_id=partner, device_id_type=MESH,
    )
    m_copy.start()
    mm[pl.ds(mine, own), :] = jnp.where(left, m_left, m_right)

    ct_copy.wait()
    totals = ct[...]
    c_parts = jnp.concatenate(split3(totals), axis=1)
    holds = jnp.concatenate([hold_m, hold_m, hold_m], axis=0)
    taken = jnp.dot(c_parts, holds, preferred_element_type=F32)
    live = 0.5 * jnp.sum(totals, axis=1, keepdims=True) - taken[:, :half] + opp[...].astype(F32)
    half_pot = 0.5 * column(pot[...])
    win = half_pot + column(bet[...] * pot[...])
    stake = half_pot * live * (1.0 / hands)

    m_copy.wait()
    value = jnp.maximum(win * mm[:, :half] * (1.0 / hands), -stake)
    bv_out[...] = value
    scale = 1.0 / (boards * nb)
    hand_part = jnp.sum(value, axis=0, keepdims=True) * scale
    mass_part = jnp.sum(stake, axis=0, keepdims=True) * scale
    tr = trav[...]
    num = jnp.sum(tr * hand_part, axis=1, keepdims=True)
    den = jnp.sum(tr * mass_part, axis=1, keepdims=True)
    lane = iota((1, halfp), 1)
    msg[...] = jnp.where(lane == halfp - 2, num, jnp.where(lane == halfp - 1, den, 0.0))
    msg[:, :half] = hand_part

    copies = []
    for k in range(nb):
        peer = lax.rem(me + k, nb)
        if k:
            copies.append(
                pltpu.make_async_remote_copy(
                    src_ref=msg, dst_ref=recva.at[k], send_sem=send_a.at[k], recv_sem=recv_a.at[k],
                    device_id=(peer, h), device_id_type=MESH,
                )
            )
        copies.append(
            pltpu.make_async_remote_copy(
                src_ref=msg.at[:, pl.ds(halfp - LANES, LANES)], dst_ref=recvb.at[k],
                send_sem=send_b.at[k], recv_sem=recv_b.at[k],
                device_id=(peer, 1 - h), device_id_type=MESH,
            )
        )
    for copy in copies:
        copy.start()
    for copy in copies:
        copy.wait()
    total = msg[...]
    tail = jnp.zeros((1, LANES), F32)
    for k in range(nb):
        if k:
            total = total + recva[k]
        tail = tail + recvb[k]
    hv_out[...] = total[:, :half]
    ends = total[:, halfp - LANES :] + tail
    spot = iota((1, LANES), 1)
    num_all = jnp.sum(jnp.where(spot == LANES - 2, ends, 0.0), axis=1, keepdims=True)
    den_all = jnp.sum(jnp.where(spot == LANES - 1, ends, 0.0), axis=1, keepdims=True)
    ex_out[...] = num_all / den_all


def solution(mesh):
    nb = mesh.shape["board"]

    def local(opp_reach, hand_rank, hand_cards, pot, bet_frac, trav_reach):
        boards, half = opp_reach.shape
        hands = hand_rank.shape[1]
        own = boards // 2
        hp = up(hands, LANES)
        halfp = up(half + 2, LANES)
        blocks = -(-(CARDS // 2) // (LANES // own))
        nhi = up(-(-hands // DIGIT), 16)
        nlo = DIGIT + 16
        vm = pltpu.VMEM
        dma = pltpu.SemaphoreType.DMA
        spec = pl.BlockSpec(memory_space=pltpu.VMEM)
        value, hand_values, ratio = pl.pallas_call(
            functools.partial(kernel, nb),
            out_shape=(
                jax.ShapeDtypeStruct((boards, half), F32),
                jax.ShapeDtypeStruct((1, half), F32),
                jax.ShapeDtypeStruct((1, 1), F32),
            ),
            in_specs=[spec] * 6,
            out_specs=(spec, spec, spec),
            scratch_shapes=[
                vm((CARDS * STRIDE, hp), BF16),
                vm((2, hp), jnp.int32),
                vm((own, hp), F32),
                vm((own, hp), F32),
                vm((own, hp), F32),
                vm((3 * own, hp), BF16),
                vm((own, half), BF16),
                vm((blocks, LANES, LANES), F32),
                vm((blocks, LANES, LANES), F32),
                vm((blocks, LANES, LANES), F32),
                vm((own, 2 * nhi, hp), BF16),
                vm((own, nlo, 2 * nhi), F32),
                vm((own, 2 * nhi), F32),
                vm((own, hp), F32),
                vm((boards, LANES), F32),
                vm((boards, halfp), F32),
                vm((own, halfp), F32),
                vm((1, halfp), F32),
                vm((nb, 1, halfp), F32),
                vm((nb, 1, LANES), F32),
                dma((2,)),
                dma((2,)),
                dma((2,)),
                dma((nb,)),
                dma((nb,)),
                dma((nb,)),
                dma((nb,)),
            ],
            compiler_params=pltpu.CompilerParams(collective_id=0, has_side_effects=True),
        )(opp_reach, hand_rank, hand_cards.T, pot[None, :], bet_frac[None, :], trav_reach[None, :])
        return value, hand_values[0], ratio[0, 0]

    placed = (P("board", "hand"), P("board", None), P(), P("board"), P("board"), P("hand"))
    return jax.shard_map(
        local,
        mesh=mesh,
        in_specs=placed,
        out_specs=(P("board", "hand"), P("hand"), P()),
        check_vma=False,
    )
```

```python
import functools

import jax
import jax.numpy as jnp
from jax import lax
from jax.experimental import pallas as pl
from jax.experimental.pallas import tpu as pltpu
from jax.sharding import PartitionSpec as P

CARDS = 52
LANES = 128
STRIDE = 64
DIGIT = 32
MESH = pl.DeviceIdType.MESH
F32 = jnp.float32
BF16 = jnp.bfloat16
NT = (((1,), (1,)), ((), ()))


def up(n, m):
    return (n + m - 1) // m * m


def iota(shape, axis, dtype=jnp.int32):
    return lax.broadcasted_iota(jnp.int32, shape, axis).astype(dtype)


def column(row):
    n = row.shape[1]
    diag = iota((n, n), 0) == iota((n, n), 1)
    return jnp.sum(jnp.where(diag, row, 0.0), axis=1, keepdims=True)


def split2(x):
    top = x.astype(BF16)
    return top, (x - top.astype(F32)).astype(BF16)


def split3(x):
    top = x.astype(BF16)
    rest = x - top.astype(F32)
    mid, low = split2(rest)
    return top, mid, low


def kernel(
    nb, opp, rank, cards, pot, bet, trav, bv_out, hv_out, ex_out,
    pt, key, rhi, rlo, wf, xs, got, tt, wt, st, eqs, c1, rt, gg, ct, mm, sb, msg, recva, recvb,
    s_reach, s_ct, s_m, send_a, recv_a, send_b, recv_b,
):
    me, h = lax.axis_index("board"), lax.axis_index("hand")
    boards, half = opp.shape
    hands = rank.shape[1]
    own = boards // 2
    hp = wf.shape[1]
    halfp = mm.shape[1]
    mine = pl.multiple_of(h * own, own)
    theirs = pl.multiple_of((1 - h) * own, own)
    partner = (me, 1 - h)
    pairs = CARDS // 2
    group = LANES // own
    blocks = tt.shape[0]
    left = h == 0

    barrier = pltpu.get_barrier_semaphore()
    for k in range(nb):
        peer = lax.rem(me + k, nb)
        if k:
            pl.semaphore_signal(barrier, inc=1, device_id=(peer, h), device_id_type=MESH)
        pl.semaphore_signal(barrier, inc=1, device_id=(peer, 1 - h), device_id_type=MESH)

    key[...] = jnp.full(key.shape, -1, jnp.int32)
    key[:, :hands] = cards[...]
    u, v = key[0:1, :], key[1:2, :]
    rows = rank[pl.ds(mine, own), :]
    rhi[...] = jnp.zeros(rhi.shape, F32)
    rlo[...] = jnp.zeros(rlo.shape, F32)
    rhi[:, :hands] = (rows // DIGIT).astype(F32)
    rlo[:, :hands] = (rows % DIGIT).astype(F32)

    depth = iota((STRIDE, hp), 0, F32).astype(BF16)

    def build(c, carry):
        other = jnp.where(u == c, v, jnp.where(v == c, u, -1)).astype(F32).astype(BF16)
        hit = depth == jnp.broadcast_to(other, (STRIDE, hp))
        start = pl.multiple_of(c * STRIDE, STRIDE)
        pt[pl.ds(start, STRIDE), :] = jnp.where(hit, jnp.ones((), BF16), jnp.zeros((), BF16))
        return carry

    lax.fori_loop(0, CARDS // 2, build, 0)

    pl.semaphore_wait(barrier, 2 * nb - 1)
    reach_copy = pltpu.make_async_remote_copy(
        src_ref=opp.at[pl.ds(theirs, own)], dst_ref=got, send_sem=s_reach.at[0], recv_sem=s_reach.at[1],
        device_id=partner, device_id_type=MESH,
    )
    reach_copy.start()
    lax.fori_loop(CARDS // 2, CARDS, build, 0)

    card_row = iota((LANES, hp), 0)
    hold = ((card_row == u) | (card_row == v)).astype(F32).astype(BF16)
    shift = hp - half
    u_r, v_r = pltpu.roll(key[...], shift, 1)[0:1, :halfp], pltpu.roll(key[...], shift, 1)[1:2, :halfp]
    u_m = jnp.where(left, u[:, :halfp], u_r)
    v_m = jnp.where(left, v[:, :halfp], v_r)
    card_half = iota((LANES, halfp), 0)
    hold_m = ((card_half == u_m) | (card_half == v_m)).astype(F32).astype(BF16)

    nhi = c1.shape[2] // 2
    hi_row = iota((nhi, hp), 0, F32).astype(BF16)

    def digit(b, carry):
        hi_b = jnp.broadcast_to(rhi[pl.ds(b, 1), :].astype(BF16), (nhi, hp))
        eq = jnp.where(hi_row == hi_b, jnp.ones((), BF16), jnp.zeros((), BF16))
        eqs[b, 0:nhi, :] = eq
        eqs[b, nhi : 2 * nhi, :] = eq
        return carry

    lax.fori_loop(0, own, digit, 0, unroll=2)

    reach_copy.wait()
    here, there = opp[pl.ds(mine, own), :].astype(F32), got[...].astype(F32)
    wf[...] = jnp.zeros(wf.shape, F32)
    wf[:, :half] = jnp.where(left, there, here)
    second = pltpu.roll(wf[...], half, 1)
    wf[...] = jnp.zeros(wf.shape, F32)
    wf[:, :half] = jnp.where(left, here, there)
    w_all = wf[...] + second
    wf[...] = w_all
    w_low = w_all.astype(BF16)

    ct[pl.ds(mine, own), :] = lax.dot_general(w_low, hold, NT, preferred_element_type=F32)
    ct_copy = pltpu.make_async_remote_copy(
        src_ref=ct.at[pl.ds(mine, own)], dst_ref=ct.at[pl.ds(mine, own)], send_sem=s_ct.at[0], recv_sem=s_ct.at[1],
        device_id=partner, device_id_type=MESH,
    )
    ct_copy.start()

    xs[0:own, :] = rhi[...].astype(BF16)
    xs[own : 2 * own, :] = rlo[...].astype(BF16)
    xs[2 * own :, :] = w_low
    table = lax.dot_general(xs[...], pt[...], NT, preferred_element_type=F32)
    t_tab = table[0:own] * float(DIGIT) + table[own : 2 * own]
    w_tab = table[2 * own :]
    for blk in range(blocks):
        for src, dst in ((t_tab, tt), (w_tab, wt)):
            parts = []
            for q in range(group):
                p = blk * group + q
                if p < pairs:
                    parts.append(src[:, p * LANES : (p + 1) * LANES])
                else:
                    parts.append(jnp.zeros((own, LANES), F32))
            dst[blk] = jnp.concatenate(parts, axis=0).T

    used = up(CARDS, 8)
    st[...] = jnp.zeros(st.shape, F32)

    def correct(n, carry):
        blk, off = n // 2, pl.multiple_of((n % 2) * STRIDE, STRIDE)
        t_here = tt[blk, pl.ds(off, used), :]
        acc = jnp.zeros((used, LANES), F32)
        for e in range(CARDS):
            te = tt[blk, pl.ds(off + e, 1), :]
            we = wt[blk, pl.ds(off + e, 1), :]
            acc = acc + jnp.where(t_here > te, we, jnp.where(t_here < te, -we, 0.0))
        st[blk, pl.ds(off, used), :] = acc
        return carry

    lax.fori_loop(0, 2 * blocks, correct, 0)
    pieces = []
    for p in range(pairs):
        blk, q = p // group, p % group
        if q == 0:
            back = st[blk].T
        pieces.append(back[q * own : (q + 1) * own])
    s_tab = jnp.concatenate(pieces, axis=1)
    s_top, s_low = split2(s_tab)
    scattered = jnp.dot(jnp.concatenate([s_top, s_low], axis=0), pt[...], preferred_element_type=F32)
    corr = scattered[:own] + scattered[own:]

    nlo = c1.shape[1]
    lo_row = iota((nlo, hp), 0, F32).astype(BF16)

    def hist(b, carry):
        lo_b = jnp.broadcast_to(rlo[pl.ds(b, 1), :].astype(BF16), (nlo, hp))
        w_b = jnp.broadcast_to(wf[pl.ds(b, 1), :].astype(BF16), (nlo, hp))
        lw = jnp.where(lo_row > lo_b, w_b, jnp.where(lo_row < lo_b, -w_b, jnp.zeros((), BF16)))
        part = lax.dot_general(lw, eqs[b], NT, preferred_element_type=F32)
        c1[b] = part
        rt[pl.ds(b, 1), :] = part[DIGIT : DIGIT + 1, :]
        return carry

    lax.fori_loop(0, own, hist, 0, unroll=4)
    wide = 2 * nhi
    a, z = iota((wide, wide), 0), iota((wide, wide), 1)
    z = jnp.where(z >= nhi, z - nhi, z)
    sgn = jnp.where(a >= nhi, 0, jnp.where(z > a, 1, jnp.where(z < a, -1, 0))).astype(F32).astype(BF16)
    r0, r1, r2 = split3(rt[...])
    rt[...] = (
        jnp.dot(r0, sgn, preferred_element_type=F32)
        + jnp.dot(r1, sgn, preferred_element_type=F32)
        + jnp.dot(r2, sgn, preferred_element_type=F32)
    )
    lo_f = iota((DIGIT, hp), 0, F32)
    first = iota((DIGIT, wide), 1) < nhi

    def pick(b, carry):
        tab = c1[b, 0:DIGIT, :] + rt[pl.ds(b, 1), :]
        top = tab.astype(BF16).astype(F32)
        lhs = jnp.where(first, top, tab - top).astype(BF16)
        d = jnp.dot(lhs, eqs[b], preferred_element_type=F32)
        hit = lo_f == rlo[pl.ds(b, 1), :]
        gg[pl.ds(b, 1), :] = jnp.sum(jnp.where(hit, d, 0.0), axis=0, keepdims=True)
        return carry

    lax.fori_loop(0, own, pick, 0, unroll=4)
    margin = gg[...] - corr

    m_left = margin[:, :halfp]
    m_right = pltpu.roll(margin, shift, 1)[:, :halfp]
    sb[...] = jnp.where(left, m_right, m_left)
    m_copy = pltpu.make_async_remote_copy(
        src_ref=sb, dst_ref=mm.at[pl.ds(mine, own)], send_sem=s_m.at[0], recv_sem=s_m.at[1],
        device_id=partner, device_id_type=MESH,
    )
    m_copy.start()
    mm[pl.ds(mine, own), :] = jnp.where(left, m_left, m_right)

    ct_copy.wait()
    totals = ct[...]
    c_parts = jnp.concatenate(split3(totals), axis=1)
    holds = jnp.concatenate([hold_m, hold_m, hold_m], axis=0)
    taken = jnp.dot(c_parts, holds, preferred_element_type=F32)
    live = 0.5 * jnp.sum(totals, axis=1, keepdims=True) - taken[:, :half] + opp[...].astype(F32)
    half_pot = 0.5 * column(pot[...])
    win = half_pot + column(bet[...] * pot[...])
    stake = half_pot * live * (1.0 / hands)

    m_copy.wait()
    value = jnp.maximum(win * mm[:, :half] * (1.0 / hands), -stake)
    bv_out[...] = value
    scale = 1.0 / (boards * nb)
    hand_part = jnp.sum(value, axis=0, keepdims=True) * scale
    mass_part = jnp.sum(stake, axis=0, keepdims=True) * scale
    tr = trav[...].reshape(1, half)
    num = jnp.sum(tr * hand_part, axis=1, keepdims=True)
    den = jnp.sum(tr * mass_part, axis=1, keepdims=True)
    lane = iota((1, halfp), 1)
    msg[...] = jnp.where(lane == halfp - 2, num, jnp.where(lane == halfp - 1, den, 0.0))
    msg[:, :half] = hand_part

    copies = []
    for k in range(nb):
        peer = lax.rem(me + k, nb)
        if k:
            copies.append(
                pltpu.make_async_remote_copy(
                    src_ref=msg, dst_ref=recva.at[k], send_sem=send_a.at[k], recv_sem=recv_a.at[k],
                    device_id=(peer, h), device_id_type=MESH,
                )
            )
        copies.append(
            pltpu.make_async_remote_copy(
                src_ref=msg.at[:, pl.ds(halfp - LANES, LANES)], dst_ref=recvb.at[k],
                send_sem=send_b.at[k], recv_sem=recv_b.at[k],
                device_id=(peer, 1 - h), device_id_type=MESH,
            )
        )
    for copy in copies:
        copy.start()
    for copy in copies:
        copy.wait()
    total = msg[...]
    tail = jnp.zeros((1, LANES), F32)
    for k in range(nb):
        if k:
            total = total + recva[k]
        tail = tail + recvb[k]
    hv_out[...] = total[:, :half].reshape(half)
    ends = total[:, halfp - LANES :] + tail
    spot = iota((1, LANES), 1)
    num_all = jnp.sum(jnp.where(spot == LANES - 2, ends, 0.0), axis=1, keepdims=True)
    den_all = jnp.sum(jnp.where(spot == LANES - 1, ends, 0.0), axis=1, keepdims=True)
    ex_out[...] = num_all / den_all


def solution(mesh):
    nb = mesh.shape["board"]

    def local(opp_reach, hand_rank, hand_cards, pot, bet_frac, trav_reach):
        boards, half = opp_reach.shape
        hands = hand_rank.shape[1]
        own = boards // 2
        hp = up(hands, LANES)
        halfp = up(half + 2, LANES)
        blocks = -(-(CARDS // 2) // (LANES // own))
        nhi = up(-(-hands // DIGIT), 16)
        nlo = DIGIT + 16
        vm = pltpu.VMEM
        dma = pltpu.SemaphoreType.DMA
        spec = pl.BlockSpec(memory_space=pltpu.VMEM)
        value, hand_values, ratio = pl.pallas_call(
            functools.partial(kernel, nb),
            out_shape=(vm((boards, half), F32), vm((half,), F32), vm((1, 1), F32)),
            in_specs=[spec] * 6,
            scratch_shapes=[
                vm((CARDS * STRIDE, hp), BF16),
                vm((2, hp), jnp.int32),
                vm((own, hp), F32),
                vm((own, hp), F32),
                vm((own, hp), F32),
                vm((3 * own, hp), BF16),
                vm((own, half), BF16),
                vm((blocks, LANES, LANES), F32),
                vm((blocks, LANES, LANES), F32),
                vm((blocks, LANES, LANES), F32),
                vm((own, 2 * nhi, hp), BF16),
                vm((own, nlo, 2 * nhi), F32),
                vm((own, 2 * nhi), F32),
                vm((own, hp), F32),
                vm((boards, LANES), F32),
                vm((boards, halfp), F32),
                vm((own, halfp), F32),
                vm((1, halfp), F32),
                vm((nb, 1, halfp), F32),
                vm((nb, 1, LANES), F32),
                dma((2,)),
                dma((2,)),
                dma((2,)),
                dma((nb,)),
                dma((nb,)),
                dma((nb,)),
                dma((nb,)),
            ],
            compiler_params=pltpu.CompilerParams(collective_id=0, has_side_effects=True),
        )(opp_reach, hand_rank, hand_cards.T, pot[None, :], bet_frac[None, :], trav_reach)
        return value, hand_values, ratio[0, 0]

    placed = (P("board", "hand"), P("board", None), P(), P("board"), P("board"), P("hand"))
    return jax.shard_map(
        local,
        mesh=mesh,
        in_specs=placed,
        out_specs=(P("board", "hand"), P("hand"), P()),
        check_vma=False,
    )
```

```python
import functools

import jax
import jax.numpy as jnp
from jax import lax
from jax.experimental import pallas as pl
from jax.experimental.pallas import tpu as pltpu
from jax.sharding import PartitionSpec as P

CARDS = 52
LANES = 128
STRIDE = 64
DIGIT = 32
MESH = pl.DeviceIdType.MESH
F32 = jnp.float32
BF16 = jnp.bfloat16
NT = (((1,), (1,)), ((), ()))


def up(n, m):
    return (n + m - 1) // m * m


def iota(shape, axis, dtype=jnp.int32):
    return lax.broadcasted_iota(jnp.int32, shape, axis).astype(dtype)


def column(row):
    n = row.shape[1]
    diag = iota((n, n), 0) == iota((n, n), 1)
    return jnp.sum(jnp.where(diag, row, 0.0), axis=1, keepdims=True)


def split2(x):
    top = x.astype(BF16)
    return top, (x - top.astype(F32)).astype(BF16)


def split3(x):
    top = x.astype(BF16)
    rest = x - top.astype(F32)
    mid, low = split2(rest)
    return top, mid, low


def kernel(
    nb, opp, rank, cards, pot, bet, trav, bv_out, hv_out, ex_out,
    pt, key, rhi, rlo, wf, xs, got, tt, wt, st, eqs, c1, rt, gg, ct, mm, sb, msg, recva, recvb,
    s_reach, s_ct, s_m, send_a, recv_a, send_b, recv_b,
):
    me, h = lax.axis_index("board"), lax.axis_index("hand")
    boards, half = opp.shape
    hands = rank.shape[1]
    own = boards // 2
    hp = wf.shape[1]
    halfp = mm.shape[1]
    mine = pl.multiple_of(h * own, own)
    theirs = pl.multiple_of((1 - h) * own, own)
    partner = (me, 1 - h)
    pairs = CARDS // 2
    group = LANES // own
    blocks = tt.shape[0]
    left = h == 0

    barrier = pltpu.get_barrier_semaphore()
    for k in range(nb):
        peer = lax.rem(me + k, nb)
        if k:
            pl.semaphore_signal(barrier, inc=1, device_id=(peer, h), device_id_type=MESH)
        pl.semaphore_signal(barrier, inc=1, device_id=(peer, 1 - h), device_id_type=MESH)

    key[...] = jnp.full(key.shape, -1, jnp.int32)
    key[:, :hands] = cards[...]
    u, v = key[0:1, :], key[1:2, :]
    rows = rank[pl.ds(mine, own), :]
    rhi[...] = jnp.zeros(rhi.shape, F32)
    rlo[...] = jnp.zeros(rlo.shape, F32)
    rhi[:, :hands] = (rows // DIGIT).astype(F32)
    rlo[:, :hands] = (rows % DIGIT).astype(F32)

    depth = iota((STRIDE, hp), 0, F32).astype(BF16)

    def build(c, carry):
        other = jnp.where(u == c, v, jnp.where(v == c, u, -1)).astype(F32).astype(BF16)
        hit = depth == jnp.broadcast_to(other, (STRIDE, hp))
        start = pl.multiple_of(c * STRIDE, STRIDE)
        pt[pl.ds(start, STRIDE), :] = jnp.where(hit, jnp.ones((), BF16), jnp.zeros((), BF16))
        return carry

    lax.fori_loop(0, CARDS // 2, build, 0)

    pl.semaphore_wait(barrier, 2 * nb - 1)
    reach_copy = pltpu.make_async_remote_copy(
        src_ref=opp.at[pl.ds(theirs, own)], dst_ref=got, send_sem=s_reach.at[0], recv_sem=s_reach.at[1],
        device_id=partner, device_id_type=MESH,
    )
    reach_copy.start()
    lax.fori_loop(CARDS // 2, CARDS, build, 0)

    card_row = iota((LANES, hp), 0)
    hold = ((card_row == u) | (card_row == v)).astype(F32).astype(BF16)
    shift = hp - half
    u_r, v_r = pltpu.roll(key[...], shift, 1)[0:1, :halfp], pltpu.roll(key[...], shift, 1)[1:2, :halfp]
    u_m = jnp.where(left, u[:, :halfp], u_r)
    v_m = jnp.where(left, v[:, :halfp], v_r)
    card_half = iota((LANES, halfp), 0)
    hold_m = ((card_half == u_m) | (card_half == v_m)).astype(F32).astype(BF16)

    nhi = c1.shape[2] // 2
    hi_row = iota((nhi, hp), 0, F32).astype(BF16)

    def digit(b, carry):
        hi_b = jnp.broadcast_to(rhi[pl.ds(b, 1), :].astype(BF16), (nhi, hp))
        eq = jnp.where(hi_row == hi_b, jnp.ones((), BF16), jnp.zeros((), BF16))
        eqs[b, 0:nhi, :] = eq
        eqs[b, nhi : 2 * nhi, :] = eq
        return carry

    lax.fori_loop(0, own, digit, 0, unroll=2)

    reach_copy.wait()
    here, there = opp[pl.ds(mine, own), :].astype(F32), got[...].astype(F32)
    wf[...] = jnp.zeros(wf.shape, F32)
    wf[:, :half] = jnp.where(left, there, here)
    second = pltpu.roll(wf[...], half, 1)
    wf[...] = jnp.zeros(wf.shape, F32)
    wf[:, :half] = jnp.where(left, here, there)
    w_all = wf[...] + second
    wf[...] = w_all
    w_low = w_all.astype(BF16)

    ct[pl.ds(mine, own), :] = lax.dot_general(w_low, hold, NT, preferred_element_type=F32)
    ct_copy = pltpu.make_async_remote_copy(
        src_ref=ct.at[pl.ds(mine, own)], dst_ref=ct.at[pl.ds(mine, own)], send_sem=s_ct.at[0], recv_sem=s_ct.at[1],
        device_id=partner, device_id_type=MESH,
    )
    ct_copy.start()

    xs[0:own, :] = rhi[...].astype(BF16)
    xs[own : 2 * own, :] = rlo[...].astype(BF16)
    xs[2 * own :, :] = w_low
    table = lax.dot_general(xs[...], pt[...], NT, preferred_element_type=F32)
    t_tab = table[0:own] * float(DIGIT) + table[own : 2 * own]
    w_tab = table[2 * own :]
    for blk in range(blocks):
        for src, dst in ((t_tab, tt), (w_tab, wt)):
            parts = []
            for q in range(group):
                p = blk * group + q
                if p < pairs:
                    parts.append(src[:, p * LANES : (p + 1) * LANES])
                else:
                    parts.append(jnp.zeros((own, LANES), F32))
            dst[blk] = jnp.concatenate(parts, axis=0).T

    used = up(CARDS, 8)
    st[...] = jnp.zeros(st.shape, F32)

    def correct(n, carry):
        blk, off = n // 2, pl.multiple_of((n % 2) * STRIDE, STRIDE)
        t_here = tt[blk, pl.ds(off, used), :]
        acc = jnp.zeros((used, LANES), F32)
        for e in range(CARDS):
            te = tt[blk, pl.ds(off + e, 1), :]
            we = wt[blk, pl.ds(off + e, 1), :]
            acc = acc + jnp.where(t_here > te, we, jnp.where(t_here < te, -we, 0.0))
        st[blk, pl.ds(off, used), :] = acc
        return carry

    lax.fori_loop(0, 2 * blocks, correct, 0)
    pieces = []
    for p in range(pairs):
        blk, q = p // group, p % group
        if q == 0:
            back = st[blk].T
        pieces.append(back[q * own : (q + 1) * own])
    s_tab = jnp.concatenate(pieces, axis=1)
    s_top, s_low = split2(s_tab)
    scattered = jnp.dot(jnp.concatenate([s_top, s_low], axis=0), pt[...], preferred_element_type=F32)
    corr = scattered[:own] + scattered[own:]

    nlo = c1.shape[1]
    lo_row = iota((nlo, hp), 0, F32).astype(BF16)

    def hist(b, carry):
        lo_b = jnp.broadcast_to(rlo[pl.ds(b, 1), :].astype(BF16), (nlo, hp))
        w_b = jnp.broadcast_to(wf[pl.ds(b, 1), :].astype(BF16), (nlo, hp))
        lw = jnp.where(lo_row > lo_b, w_b, jnp.where(lo_row < lo_b, -w_b, jnp.zeros((), BF16)))
        part = lax.dot_general(lw, eqs[b], NT, preferred_element_type=F32)
        c1[b] = part
        rt[pl.ds(b, 1), :] = part[DIGIT : DIGIT + 1, :]
        return carry

    lax.fori_loop(0, own, hist, 0, unroll=8)
    wide = 2 * nhi
    a, z = iota((wide, wide), 0), iota((wide, wide), 1)
    z = jnp.where(z >= nhi, z - nhi, z)
    sgn = jnp.where(a >= nhi, 0, jnp.where(z > a, 1, jnp.where(z < a, -1, 0))).astype(F32).astype(BF16)
    r0, r1, r2 = split3(rt[...])
    rt[...] = (
        jnp.dot(r0, sgn, preferred_element_type=F32)
        + jnp.dot(r1, sgn, preferred_element_type=F32)
        + jnp.dot(r2, sgn, preferred_element_type=F32)
    )
    lo_f = iota((DIGIT, hp), 0, F32)
    first = iota((DIGIT, wide), 1) < nhi

    def pick(b, carry):
        tab = c1[b, 0:DIGIT, :] + rt[pl.ds(b, 1), :]
        top = tab.astype(BF16).astype(F32)
        lhs = jnp.where(first, top, tab - top).astype(BF16)
        d = jnp.dot(lhs, eqs[b], preferred_element_type=F32)
        hit = lo_f == rlo[pl.ds(b, 1), :]
        gg[pl.ds(b, 1), :] = jnp.sum(jnp.where(hit, d, 0.0), axis=0, keepdims=True)
        return carry

    lax.fori_loop(0, own, pick, 0, unroll=8)
    margin = gg[...] - corr

    m_left = margin[:, :halfp]
    m_right = pltpu.roll(margin, shift, 1)[:, :halfp]
    sb[...] = jnp.where(left, m_right, m_left)
    m_copy = pltpu.make_async_remote_copy(
        src_ref=sb, dst_ref=mm.at[pl.ds(mine, own)], send_sem=s_m.at[0], recv_sem=s_m.at[1],
        device_id=partner, device_id_type=MESH,
    )
    m_copy.start()
    mm[pl.ds(mine, own), :] = jnp.where(left, m_left, m_right)

    ct_copy.wait()
    totals = ct[...]
    c_parts = jnp.concatenate(split3(totals), axis=1)
    holds = jnp.concatenate([hold_m, hold_m, hold_m], axis=0)
    taken = jnp.dot(c_parts, holds, preferred_element_type=F32)
    live = 0.5 * jnp.sum(totals, axis=1, keepdims=True) - taken[:, :half] + opp[...].astype(F32)
    half_pot = 0.5 * column(pot[...])
    win = half_pot + column(bet[...] * pot[...])
    stake = half_pot * live * (1.0 / hands)

    m_copy.wait()
    value = jnp.maximum(win * mm[:, :half] * (1.0 / hands), -stake)
    bv_out[...] = value
    scale = 1.0 / (boards * nb)
    hand_part = jnp.sum(value, axis=0, keepdims=True) * scale
    mass_part = jnp.sum(stake, axis=0, keepdims=True) * scale
    tr = trav[...].reshape(1, half)
    num = jnp.sum(tr * hand_part, axis=1, keepdims=True)
    den = jnp.sum(tr * mass_part, axis=1, keepdims=True)
    lane = iota((1, halfp), 1)
    msg[...] = jnp.where(lane == halfp - 2, num, jnp.where(lane == halfp - 1, den, 0.0))
    msg[:, :half] = hand_part

    copies = []
    for k in range(nb):
        peer = lax.rem(me + k, nb)
        if k:
            copies.append(
                pltpu.make_async_remote_copy(
                    src_ref=msg, dst_ref=recva.at[k], send_sem=send_a.at[k], recv_sem=recv_a.at[k],
                    device_id=(peer, h), device_id_type=MESH,
                )
            )
        copies.append(
            pltpu.make_async_remote_copy(
                src_ref=msg.at[:, pl.ds(halfp - LANES, LANES)], dst_ref=recvb.at[k],
                send_sem=send_b.at[k], recv_sem=recv_b.at[k],
                device_id=(peer, 1 - h), device_id_type=MESH,
            )
        )
    for copy in copies:
        copy.start()
    for copy in copies:
        copy.wait()
    total = msg[...]
    tail = jnp.zeros((1, LANES), F32)
    for k in range(nb):
        if k:
            total = total + recva[k]
        tail = tail + recvb[k]
    hv_out[...] = total[:, :half].reshape(half)
    ends = total[:, halfp - LANES :] + tail
    spot = iota((1, LANES), 1)
    num_all = jnp.sum(jnp.where(spot == LANES - 2, ends, 0.0), axis=1, keepdims=True)
    den_all = jnp.sum(jnp.where(spot == LANES - 1, ends, 0.0), axis=1, keepdims=True)
    ex_out[...] = num_all / den_all


def solution(mesh):
    nb = mesh.shape["board"]

    def local(opp_reach, hand_rank, hand_cards, pot, bet_frac, trav_reach):
        boards, half = opp_reach.shape
        hands = hand_rank.shape[1]
        own = boards // 2
        hp = up(hands, LANES)
        halfp = up(half + 2, LANES)
        blocks = -(-(CARDS // 2) // (LANES // own))
        nhi = up(-(-hands // DIGIT), 16)
        nlo = DIGIT + 16
        vm = pltpu.VMEM
        dma = pltpu.SemaphoreType.DMA
        spec = pl.BlockSpec(memory_space=pltpu.VMEM)
        value, hand_values, ratio = pl.pallas_call(
            functools.partial(kernel, nb),
            out_shape=(vm((boards, half), F32), vm((half,), F32), vm((1, 1), F32)),
            in_specs=[spec] * 6,
            scratch_shapes=[
                vm((CARDS * STRIDE, hp), BF16),
                vm((2, hp), jnp.int32),
                vm((own, hp), F32),
                vm((own, hp), F32),
                vm((own, hp), F32),
                vm((3 * own, hp), BF16),
                vm((own, half), BF16),
                vm((blocks, LANES, LANES), F32),
                vm((blocks, LANES, LANES), F32),
                vm((blocks, LANES, LANES), F32),
                vm((own, 2 * nhi, hp), BF16),
                vm((own, nlo, 2 * nhi), F32),
                vm((own, 2 * nhi), F32),
                vm((own, hp), F32),
                vm((boards, LANES), F32),
                vm((boards, halfp), F32),
                vm((own, halfp), F32),
                vm((1, halfp), F32),
                vm((nb, 1, halfp), F32),
                vm((nb, 1, LANES), F32),
                dma((2,)),
                dma((2,)),
                dma((2,)),
                dma((nb,)),
                dma((nb,)),
                dma((nb,)),
                dma((nb,)),
            ],
            compiler_params=pltpu.CompilerParams(collective_id=0, has_side_effects=True),
        )(opp_reach, hand_rank, hand_cards.T, pot[None, :], bet_frac[None, :], trav_reach)
        return value, hand_values, ratio[0, 0]

    placed = (P("board", "hand"), P("board", None), P(), P("board"), P("board"), P("hand"))
    return jax.shard_map(
        local,
        mesh=mesh,
        in_specs=placed,
        out_specs=(P("board", "hand"), P("hand"), P()),
        check_vma=False,
    )
```
